32 devices in a mesh: batch: 16 (over z, x, core), chan: 2 (over y).
Axes of the slice: x: 2, y: 2, z: 4, core: 2. Of those that a mesh axis runs over, the one named last changes fastest.
Arguments:
- audio: bfloat16 [32, 256, 2048], P('batch', 'chan'), may hold values from -6 to 6
- lengths: int32 [32], P('batch'), may hold values from 1 to 256, 5120 in all
- codes: int32 [32, 2, 2, 256], P('batch', 'chan'), may hold values from 0 to 1023
- enc_wide: bfloat16 [3, 7, 256, 256], P(None, None, 'chan'), may hold values from -0.125 to 0.125
- enc_wide_bias: bfloat16 [3, 256], P(None, 'chan'), may hold values from -2 to 2
- enc_point: bfloat16 [3, 256, 256], P(None, 'chan'), may hold values from -0.375 to 0.375
- enc_point_bias: bfloat16 [3, 256], P(None, 'chan'), may hold values from -2 to 2
- down_weight: bfloat16 [16, 512, 256], P(None, 'chan'), may hold values from -0.09375 to 0.09375
- down_bias: bfloat16 [512], P('chan'), may hold values from -2 to 2
- codebooks: float32 [2, 2, 1024, 256], P('chan'), may hold values from -4 to 4
- up_weight: bfloat16 [16, 256, 512], P(None, 'chan'), may hold values from -0.1875 to 0.1875
- up_bias: bfloat16 [256], P('chan'), may hold values from -2 to 2
- dec_wide: bfloat16 [3, 7, 256, 256], P(None, None, 'chan'), may hold values from -0.125 to 0.125
- dec_wide_bias: bfloat16 [3, 256], P(None, 'chan'), may hold values from -2 to 2
- dec_point: bfloat16 [3, 256, 256], P(None, 'chan'), may hold values from -0.375 to 0.375
- dec_point_bias: bfloat16 [3, 256], P(None, 'chan'), may hold values from -2 to 2
- cotangent: bfloat16 [32, 256, 2048], P('batch', 'chan'), may hold values from -6 to 6
Outputs:
- output: bfloat16 [32, 256, 2048], P('batch', 'chan')
- audio_grad: float32 [32, 256, 2048], P('batch', 'chan')
- enc_wide_grad: float32 [3, 7, 256, 256], P(None, None, 'chan')
- enc_wide_bias_grad: float32 [3, 256], P(None, 'chan')
- enc_point_grad: float32 [3, 256, 256], P(None, 'chan')
- enc_point_bias_grad: float32 [3, 256], P(None, 'chan')
- down_weight_grad: float32 [16, 512, 256], P(None, 'chan')
- down_bias_grad: float32 [512], P('chan')
- codebooks_grad: float32 [2, 2, 1024, 256], P('chan')
- up_weight_grad: float32 [16, 256, 512], P(None, 'chan')
- up_bias_grad: float32 [256], P('chan')
- dec_wide_grad: float32 [3, 7, 256, 256], P(None, None, 'chan')
- dec_wide_bias_grad: float32 [3, 256], P(None, 'chan')
- dec_point_grad: float32 [3, 256, 256], P(None, 'chan')
- dec_point_bias_grad: float32 [3, 256], P(None, 'chan')
The draws below stay inside these ranges and needn't reach their ends.
Inputs may be any that keep to these rules, and one draw needn't show every extreme that they name: lengths of all 32 clips sum to 5120 latent frames and some clip is 256 frames long.
All inputs are finite; a program needn't handle non-finite values. No bound on the sum of `lengths` on one device may be relied on, other than what follows from the above.
Results may differ from the reference program's by a relative error of at most 0.018.
Values may be sent and summed in bfloat16 or wider, within the bound.
No kernel may reach another device: no remote copies, remote signals or barrier semaphores. Data moves between devices by JAX's collectives and lax.ppermute only.
A program may use at most 320 MiB of HBM per device.

```python
import math
import jax
import jax.numpy as jnp
import numpy as np
from jax import lax

C = 256
Z = 512
GROUPS = 2
LEVELS = 2
CODES = 1024
TAPS = 7
STRIDE = 8
UNITS = 3
CLIPS_DEV = 2
MAXLAT = 256
GW = 256
TIME = 2048
CLIPS = 32


def with_ends(array, rng, smallest, top_value):
    place = [jax.random.randint(jax.random.fold_in(rng, axis), (), 0, length) for axis, length in enumerate(array.shape)]
    longest = array.shape.index(max(array.shape))
    next_to = place[:longest] + [(place[longest] + 1) % array.shape[longest]] + place[longest + 1:]
    return array.at[tuple(place)].set(smallest).at[tuple(next_to)].set(top_value)


def level_of(stream_key, dims, cuts, least, largest):
    gain = 1.0
    for position, blocks in cuts:
        draws = jax.random.uniform(jax.random.fold_in(jax.random.fold_in(stream_key, 6), position), (blocks,), jnp.float32, least / len(cuts), largest / len(cuts))
        gain = gain * jnp.repeat(jnp.exp(draws), dims[position] // blocks).reshape((-1,) + (1,) * (len(dims) - 1 - position))
    return gain


def split_up(count, total, bound, slope):
    portions = [(1 << 20) // math.isqrt(rank ** slope) + 1 for rank in range(2, count + 1)]
    spare, counts = total - bound - (count - 1), [1] * (count - 1)
    while spare > 0:
        candidates = [i for i in range(count - 1) if counts[i] < bound]
        pool, budget = sum([portions[i] for i in candidates]), spare
        for i in candidates:
            more = min(bound - counts[i], max(1, budget * portions[i] // pool), spare)
            counts[i] = counts[i] + more
            spare = spare - more
    return np.array([bound] + counts)


def ragged_sizes(key, number_of, total, limit, skew):
    if number_of == 2:
        one = jax.random.randint(key, (), max(1, total - limit), min(limit, total - 1) + 1)
        return jnp.stack([one, total - one])
    tallies = jnp.asarray(split_up(number_of, total, limit, skew), jnp.int32)
    twos = (number_of - 1) // 2
    source_of, receiver = tallies[1:1 + 2 * twos:2], tallies[2:2 + 2 * twos:2]
    room = jnp.minimum(source_of - 1, limit - receiver)
    moved = jax.random.randint(jax.random.fold_in(key, 1), (twos,), 0, 1 << 20) % (room + 1)
    tallies = tallies.at[1:1 + 2 * twos:2].set(source_of - moved).at[2:2 + 2 * twos:2].set(receiver + moved)
    return tallies[jax.random.permutation(jax.random.fold_in(key, 2), number_of)]


def centred(key, shape, width, bound, cuts=(), held_as=jnp.bfloat16):
    drawn = jax.random.normal(key, shape, jnp.float32) * width
    if len(cuts) > 0:
        drawn = level_of(key, shape, cuts, -0.22, 0.18) * drawn
    return jnp.clip(drawn, min=-bound, max=bound).astype(held_as)


def setup_inputs(seed: int = 0) -> dict:
    key_list = jax.random.split(jax.random.key(seed), 18)
    return {
        "audio": centred(key_list[0], (CLIPS, C, TIME), 1.0, 6.0, ((0, 16), (1, 2))),
        "lengths": ragged_sizes(key_list[1], CLIPS, CLIPS * MAXLAT * 5 // 8, MAXLAT, 2).astype(jnp.int32),
        "codes": with_ends(jax.random.randint(key_list[2], (CLIPS, GROUPS, LEVELS, MAXLAT), 0, CODES), jax.random.fold_in(key_list[2], 1), 0, CODES - 1).astype(jnp.int32),
        "enc_wide": centred(key_list[3], (UNITS, TAPS, C, C), (TAPS * C) ** -0.5, 0.125, ((2, 2),)),
        "enc_wide_bias": centred(key_list[4], (UNITS, C), 0.3, 2.0, ((1, 2),)),
        "enc_point": centred(key_list[5], (UNITS, C, C), C ** -0.5, 0.375, ((1, 2),)),
        "enc_point_bias": centred(key_list[6], (UNITS, C), 0.3, 2.0, ((1, 2),)),
        "down_weight": centred(key_list[7], (2 * STRIDE, Z, C), (2 * STRIDE * C) ** -0.5, 0.09375, ((1, 2),)),
        "down_bias": centred(key_list[8], (Z,), 0.3, 2.0, ((0, 2),)),
        "codebooks": centred(key_list[9], (GROUPS, LEVELS, CODES, GW), 0.7, 4.0, ((0, 2),), jnp.float32),
        "up_weight": centred(key_list[10], (2 * STRIDE, C, Z), (2 * Z) ** -0.5, 0.1875, ((1, 2),)),
        "up_bias": centred(key_list[11], (C,), 0.3, 2.0, ((0, 2),)),
        "dec_wide": centred(key_list[12], (UNITS, TAPS, C, C), (TAPS * C) ** -0.5, 0.125, ((2, 2),)),
        "dec_wide_bias": centred(key_list[13], (UNITS, C), 0.3, 2.0, ((1, 2),)),
        "dec_point": centred(key_list[14], (UNITS, C, C), C ** -0.5, 0.375, ((1, 2),)),
        "dec_point_bias": centred(key_list[15], (UNITS, C), 0.3, 2.0, ((1, 2),)),
        "cotangent": centred(key_list[16], (CLIPS, C, TIME), 1.0, 6.0, ((0, 16), (1, 2))),
    }


BETA = 0.25
DILATIONS = (1, 3, 9)
HIGHEST = lax.Precision.HIGHEST

@jax.custom_vjp
def low(v):
    return lax.optimization_barrier(v.astype(jnp.bfloat16)).astype(jnp.float32)

@jax.custom_vjp
def low_back(v):
    return v

def low_keep(v):
    return (low(v), None)

def low_pass(kept, grad):
    return (grad,)

def back_keep(v):
    return (v, None)

def back_low(kept, grad):
    return (low(grad),)
low.defvjp(low_keep, low_pass)
low_back.defvjp(back_keep, back_low)

def shifted(values, offset):
    if offset == 0:
        return values
    length_t = values.shape[-1]
    filler = jnp.zeros(values.shape[:-1] + (abs(offset),), values.dtype)
    if offset > 0:
        return jnp.concatenate([values[..., offset:], filler], axis=-1)
    return jnp.concatenate([filler, values[..., :length_t + offset]], axis=-1)

def taps_apply(act, weight, dilation):
    center = weight.shape[0] // 2
    summed = jnp.einsum('oi,bit->bot', weight[0], shifted(act, -center * dilation), precision=HIGHEST)
    for tap_index in range(1, weight.shape[0]):
        summed = summed + jnp.einsum('oi,bit->bot', weight[tap_index], shifted(act, (tap_index - center) * dilation), precision=HIGHEST)
    return summed

def strided_apply(act, weight):
    batch_n, chans, length_t = act.shape
    blocks_now = act.reshape(batch_n, chans, length_t // STRIDE, STRIDE)
    following = jnp.concatenate([blocks_now[:, :, 1:], jnp.zeros_like(blocks_now[:, :, :1])], axis=2)
    return jnp.einsum('koi,bijk->boj', weight[:STRIDE], blocks_now, precision=HIGHEST) + jnp.einsum('koi,bijk->boj', weight[STRIDE:], following, precision=HIGHEST)

def spread_apply(act, weight):
    batch_n, chans, latent_len = act.shape
    previous = jnp.concatenate([jnp.zeros_like(act[..., :1]), act[..., :-1]], axis=-1)
    result = jnp.einsum('koi,bij->bojk', weight[:STRIDE], act, precision=HIGHEST) + jnp.einsum('koi,bij->bojk', weight[STRIDE:], previous, precision=HIGHEST)
    return result.reshape(batch_n, weight.shape[1], latent_len * STRIDE)

def res_unit(hidden, wide_w, wide_b, point_w, point_b, mask_time, dilation):
    first = low(jax.nn.elu(hidden))
    inner = mask_time * (low_back(taps_apply(first, wide_w, dilation)) + wide_b[None, :, None])
    second = low(jax.nn.elu(inner))
    outer = mask_time * (low_back(taps_apply(second, point_w[None], 1)) + point_b[None, :, None])
    return hidden + outer

def encode(audio_in, mask_time, mask_lat, wide_w, wide_b, point_w, point_b, down_w, down_b):
    hidden = mask_time * audio_in
    for unit_index in range(UNITS):
        hidden = res_unit(hidden, wide_w[unit_index], wide_b[unit_index], point_w[unit_index], point_b[unit_index], mask_time, DILATIONS[unit_index])
    act = low(jax.nn.elu(hidden))
    return mask_lat * (low_back(strided_apply(act, down_w)) + down_b[None, :, None])

def lookup(books, one_hot, level_index):
    return jnp.einsum('bgjc,gcw->bgwj', one_hot[:, :, level_index], books[:, level_index], precision=HIGHEST)

def reference(audio, lengths, codes, enc_wide, enc_wide_bias, enc_point, enc_point_bias, down_weight, down_bias, codebooks, up_weight, up_bias, dec_wide, dec_wide_bias, dec_point, dec_point_bias, cotangent):
    group_count = CLIPS // CLIPS_DEV
    params = tuple((item.astype(jnp.float32) for item in (enc_wide, enc_wide_bias, enc_point, enc_point_bias, down_weight, down_bias, codebooks, up_weight, up_bias, dec_wide, dec_wide_bias, dec_point, dec_point_bias)))

    def one_group(carry, inputs):
        audio_g, lengths_g, codes_g, cot_g = inputs
        frames = jnp.arange(MAXLAT, dtype=jnp.int32)
        mask_lat = (frames[None, None, :] < lengths_g[:, None, None]).astype(jnp.float32)
        samples = jnp.arange(TIME, dtype=jnp.int32)
        mask_time = (samples[None, None, :] < STRIDE * lengths_g[:, None, None]).astype(jnp.float32)
        mask_group = mask_lat[:, :, None, :]
        one_hot = (codes_g[..., None] == jnp.arange(CODES, dtype=jnp.int32)).astype(jnp.float32)
        audio_in = audio_g.astype(jnp.float32)
        latent_fixed = encode(audio_in, mask_time, mask_lat, *params[:6]).reshape(CLIPS_DEV, GROUPS, GW, MAXLAT)
        quant_fixed = [lookup(params[6], one_hot, level_index) for level_index in range(LEVELS)]
        shift_fixed = mask_group * sum(quant_fixed) - latent_fixed

        def forward(audio_x, wide_w, wide_b, point_w, point_b, down_w, down_b, books, up_w, up_b, dwide_w, dwide_b, dpoint_w, dpoint_b):
            latent = encode(audio_x, mask_time, mask_lat, wide_w, wide_b, point_w, point_b, down_w, down_b)
            grouped = latent.reshape(CLIPS_DEV, GROUPS, GW, MAXLAT)
            quants = [lookup(books, one_hot, level_index) for level_index in range(LEVELS)]
            residual = grouped
            residual_fixed = latent_fixed
            loss = jnp.zeros((), jnp.float32)
            for level_index in range(LEVELS):
                loss = loss + jnp.sum(mask_group * (BETA * (residual - quant_fixed[level_index]) ** 2 + (residual_fixed - quants[level_index]) ** 2))
                residual = residual - quant_fixed[level_index]
                residual_fixed = residual_fixed - quant_fixed[level_index]
            quantized = (grouped + shift_fixed).reshape(CLIPS_DEV, Z, MAXLAT)
            dec_in = low(jax.nn.elu(quantized))
            hidden = mask_time * (low_back(spread_apply(dec_in, up_w)) + up_b[None, :, None])
            for unit_index in range(UNITS):
                hidden = res_unit(hidden, dwide_w[unit_index], dwide_b[unit_index], dpoint_w[unit_index], dpoint_b[unit_index], mask_time, DILATIONS[unit_index])
            return (hidden, loss)
        outputs, pullback = jax.vjp(forward, audio_in, *params)
        grads = pullback((cot_g.astype(jnp.float32), jnp.ones((), jnp.float32)))
        updated = tuple((running + update for running, update in zip(carry, grads[1:])))
        return (updated, (outputs[0].astype(jnp.bfloat16), grads[0]))
    initial = tuple((jnp.zeros(item.shape, jnp.float32) for item in params))
    inputs = (audio.reshape(group_count, CLIPS_DEV, C, TIME), lengths.reshape(group_count, CLIPS_DEV), codes.reshape(group_count, CLIPS_DEV, GROUPS, LEVELS, MAXLAT), cotangent.reshape(group_count, CLIPS_DEV, C, TIME))
    summed, (outs_y, outs_grad) = lax.scan(one_group, initial, inputs)
    return (outs_y.reshape(CLIPS, C, TIME), outs_grad.reshape(CLIPS, C, TIME), summed[0], summed[1], summed[2], summed[3], summed[4], summed[5], summed[6], summed[7], summed[8], summed[9], summed[10], summed[11], summed[12])
```

```python
import functools

import jax
import jax.numpy as jnp
from jax import lax
from jax.experimental import pallas as pl
from jax.experimental.pallas import tpu as pltpu
from jax.sharding import PartitionSpec as P

BF = jnp.bfloat16
F32 = jnp.float32
UNITS = 3
TAPS = 7
STRIDE = 8
LEVELS = 2
DILATIONS = (1, 3, 9)
BETA = 0.25
HALO = 32
BLOCK = 512


def elu(v):
    return jnp.where(v > 0, v, jnp.exp(jnp.minimum(v, 0.0)) - 1.0)


def slope(kept):
    kept = kept.astype(F32)
    return jnp.where(kept > 0, 1.0, kept + 1.0)


def dot_nn(a, b):
    return lax.dot_general(a, b, (((1,), (0,)), ((), ())), preferred_element_type=F32)


def dot_nt(a, b):
    return lax.dot_general(a, b, (((1,), (1,)), ((), ())), preferred_element_type=F32)


def dot_tn(a, b):
    return lax.dot_general(a, b, (((0,), (0,)), ((), ())), preferred_element_type=F32)


def row_mask(start, rows, limit):
    at = start + lax.broadcasted_iota(jnp.int32, (rows, 1), 0)
    return (at < limit).astype(F32)


def assemble(sm, full, rows, own, pieces, sem):
    y, q = sm[0], sm[1]
    copies = []
    first = 0
    for ref in own:
        count = ref.shape[0]
        copies.append(
            (ref, full.at[pl.ds(first, count), pl.ds(pl.multiple_of(y * rows, rows), rows), :])
        )
        first += count
    quarter = rows // 4
    for index, ref in enumerate(pieces):
        at = (1 - y) * rows + (q ^ index) * quarter
        copies.append((ref, full.at[:, pl.ds(pl.multiple_of(at, quarter), quarter), :]))
    started = []
    for index, (src, dst) in enumerate(copies):
        copy = pltpu.make_async_copy(src, dst, sem.at[index])
        copy.start()
        started.append(copy)
    return started


def halves(y, own, other):
    return jnp.where(y == 0, own, other), jnp.where(y == 0, other, own)


def get(stream, at):
    return jnp.concatenate([stream[0, at, :], stream[1, at, :]], axis=1)


def put(stream, at, value):
    half = stream.shape[2]
    stream[0, at, :] = value[:, :half]
    stream[1, at, :] = value[:, half:]


def load_clip(y, mine, other, dst, masked, limit):
    half = other.shape[0]
    for block in range(other.shape[1] // BLOCK):
        at = pl.ds(block * BLOCK, BLOCK)
        a = mine[y, :, at].astype(F32).T
        b = other[:, at].astype(F32).T
        low, high = halves(y, a, b)
        if masked:
            mask = row_mask(block * BLOCK, BLOCK, limit)
            low, high = low * mask, high * mask
        dst[0, at, :] = low
        dst[1, at, :] = high


def zero_halo(ref, length):
    zero = jnp.zeros((HALO, ref.shape[-1]), ref.dtype)
    ref[pl.ds(0, HALO), :] = zero
    ref[pl.ds(HALO + length, HALO), :] = zero


def units_forward(limit, hidden, weight, bias, wide_row, point_row, acts, seconds, final):
    length = hidden.shape[1]
    for u in range(UNITS):
        zero_halo(acts.at[u], length)

    def first(t, carry):
        t0 = pl.multiple_of(t * BLOCK, BLOCK)
        acts[0, pl.ds(HALO + t0, BLOCK), :] = elu(get(hidden, pl.ds(t0, BLOCK))).astype(BF)
        return carry

    lax.fori_loop(0, length // BLOCK, first, 0)
    for u in range(UNITS):
        dilation = DILATIONS[u]

        def step(t, carry):
            t0 = pl.multiple_of(t * BLOCK, BLOCK)
            mask = row_mask(t0, BLOCK, limit)
            window = acts.at[u, pl.ds(t0, BLOCK + 2 * HALO), :]
            acc = bias[wide_row + u : wide_row + u + 1, :]
            for k in range(TAPS):
                x = window[pl.ds(HALO + (k - 3) * dilation, BLOCK), :]
                acc = acc + dot_nt(x, weight[u * TAPS + k])
            second = elu(mask * acc).astype(BF)
            seconds[u, pl.ds(t0, BLOCK), :] = second
            outer = dot_nt(second, weight[UNITS * TAPS + u])
            outer = mask * (outer + bias[point_row + u : point_row + u + 1, :])
            new = get(hidden, pl.ds(t0, BLOCK)) + outer
            if u + 1 < UNITS:
                acts[u + 1, pl.ds(HALO + t0, BLOCK), :] = elu(new).astype(BF)
                put(hidden, pl.ds(t0, BLOCK), new)
            else:
                put(hidden, pl.ds(t0, BLOCK), final(new))
            return carry

        lax.fori_loop(0, length // BLOCK, step, 0)


def unit_backward(u, limit, grad, weight, acts, seconds, low_out, low_in, pack, bias_out):
    _, length, half = grad.shape
    chans = 2 * half
    dilation = DILATIONS[u]

    def outer(t, carry):
        wide_sum, point_sum = carry
        t0 = pl.multiple_of(t * BLOCK, BLOCK)
        mask = row_mask(t0, BLOCK, limit)
        masked = mask * get(grad, pl.ds(t0, BLOCK))
        point_sum = point_sum + jnp.sum(masked, axis=0, keepdims=True)
        q = masked.astype(BF)
        low_out[pl.ds(t0, BLOCK), :] = q
        inner = dot_nn(q, weight[UNITS * TAPS + u])
        inner = mask * (inner * slope(seconds[u, pl.ds(t0, BLOCK), :]))
        wide_sum = wide_sum + jnp.sum(inner, axis=0, keepdims=True)
        low_in[pl.ds(HALO + t0, BLOCK), :] = inner.astype(BF)
        return wide_sum, point_sum

    zero = jnp.zeros((1, chans), F32)
    wide_sum, point_sum = lax.fori_loop(0, length // BLOCK, outer, (zero, zero))
    bias_out[u : u + 1, :] = wide_sum
    bias_out[UNITS + u : UNITS + u + 1, :] = point_sum

    def inner(t, carry):
        t0 = pl.multiple_of(t * BLOCK, BLOCK)
        window = low_in.at[pl.ds(t0, BLOCK + 2 * HALO), :]
        acc = None
        for k in range(TAPS):
            r = window[pl.ds(HALO - (k - 3) * dilation, BLOCK), :]
            part = dot_nn(r, weight[u * TAPS + k])
            acc = part if acc is None else acc + part
        kept = acts[u, pl.ds(HALO + t0, BLOCK), :]
        at = pl.ds(t0, BLOCK)
        put(grad, at, get(grad, at) + acc * slope(kept))
        return carry

    lax.fori_loop(0, length // BLOCK, inner, 0)

    def emit(index, value):
        value = value.astype(BF)
        pack[0, index] = value[:half]
        pack[1, index] = value[half:]

    emit(UNITS * TAPS + u, dot_tn(low_out[...], seconds[u]))
    for k in range(TAPS):
        x = acts[u, pl.ds(HALO + (k - 3) * dilation, length), :]
        emit(u * TAPS + k, dot_tn(low_in[pl.ds(HALO, length), :], x))


def lookup_kernel(sm, codes, books, quants, sent):
    count = books.shape[1]
    width = books.shape[2]
    frames = codes.shape[-1]
    ids = lax.broadcasted_iota(jnp.int32, (count, frames), 0)
    sums = [None, None]
    for level in range(LEVELS):
        book = books[level]
        high = book.astype(BF)
        rest = book - high.astype(F32)
        middle = rest.astype(BF)
        low = (rest - middle.astype(F32)).astype(BF)
        parts = jnp.concatenate([high, middle, low], axis=1)
        for clip in range(2):
            hot = jnp.where(ids == codes[clip, level : level + 1, :], 1.0, 0.0).astype(BF)
            found = dot_tn(hot, parts)
            quant = (
                found[:, :width] + found[:, width : 2 * width] + found[:, 2 * width :]
            )
            quants[clip, level] = quant
            sums[clip] = quant if level == 0 else (sums[clip], quant)
    for clip in range(2):
        first, second = sums[clip]
        mask = row_mask(0, frames, sm[3 + clip])
        sent[clip, :, :width] = elu(mask * (first + second)).astype(BF)
        sent[clip, :, width:] = (first + 0.5 * second).astype(BF)


def encoder_forward_kernel(
    sm, mine, other, bias, wide, point, p0, p1, p2, p3, acts, seconds, frames, weight, hidden, sem
):
    y, limit = sm[0], STRIDE * sm[2]
    copies = assemble(sm, weight, wide.shape[1], (wide, point), (p0, p1, p2, p3), sem)
    load_clip(y, mine, other, hidden, True, limit)
    for copy in copies:
        copy.wait()
    units_forward(
        limit, hidden, weight, bias, 0, 3, acts, seconds, lambda v: elu(v).astype(BF).astype(F32)
    )
    count, chans = frames.shape[0], 2 * hidden.shape[2]
    for k in range(STRIDE):
        value = get(hidden, pl.ds(k, count, stride=STRIDE))
        frames[:, k * chans : (k + 1) * chans] = value.astype(BF)


def shift_down(pad, value):
    rows, cols = value.shape
    pad[0:8, :] = jnp.zeros((8, cols), F32)
    pad[8 : 8 + rows, :] = value
    return pad[7 : 7 + rows, :]


def shift_up(pad, value):
    rows, cols = value.shape
    pad[rows : rows + 8, :] = jnp.zeros((8, cols), F32)
    pad[0:rows, :] = value
    return pad[1 : 1 + rows, :]


def decoder_forward_kernel(
    sm, e_mine, e_other, bias, up_own, u0, u1, u2, u3, wide, point, p0, p1, p2, p3,
    acts, seconds, out_own, out_sent, up_weight, weight, hidden, pad, up_sem, sem,
):
    y, limit = sm[0], STRIDE * sm[2]
    up_copies = assemble(sm, up_weight, up_own.shape[1], (up_own,), (u0, u1, u2, u3), up_sem)
    copies = assemble(sm, weight, wide.shape[1], (wide, point), (p0, p1, p2, p3), sem)
    width = e_other.shape[1] // 2
    frames = e_other.shape[0]
    low, high = halves(y, e_mine[y, :, :width].astype(F32), e_other[:, :width].astype(F32))
    e = jnp.concatenate([low, high], axis=1)
    before = shift_down(pad, e).astype(BF)
    e = e.astype(BF)
    mask = row_mask(0, frames, sm[2])
    for copy in up_copies:
        copy.wait()
    for k in range(STRIDE):
        value = dot_nt(e, up_weight[k]) + dot_nt(before, up_weight[STRIDE + k])
        put(hidden, pl.ds(k, frames, stride=STRIDE), mask * (value + bias[12:13, :]))
    for copy in copies:
        copy.wait()
    units_forward(limit, hidden, weight, bias, 6, 9, acts, seconds, lambda v: v)
    for block in range(hidden.shape[1] // BLOCK):
        at = pl.ds(block * BLOCK, BLOCK)
        own, sent = halves(y, hidden[0, at, :].T, hidden[1, at, :].T)
        out_own[:, at] = own.astype(BF)
        out_sent[:, at] = sent.astype(BF)


def decoder_backward_kernel(
    sm, mine, other, acts, seconds, wide, point, p0, p1, p2, p3,
    pack, bias_out, frames, weight, grad, low_out, low_in, sem,
):
    y, limit = sm[0], STRIDE * sm[2]
    copies = assemble(sm, weight, wide.shape[1], (wide, point), (p0, p1, p2, p3), sem)
    load_clip(y, mine, other, grad, False, limit)
    _, length, half = grad.shape
    chans = 2 * half
    zero_halo(low_in, length)
    bias_out[...] = jnp.zeros(bias_out.shape, F32)
    for copy in copies:
        copy.wait()
    for u in reversed(range(UNITS)):
        unit_backward(u, limit, grad, weight, acts, seconds, low_out, low_in, pack, bias_out)
    count = frames.shape[0]
    mask = row_mask(0, count, sm[2])
    total = jnp.zeros((1, chans), F32)
    for k in range(STRIDE):
        value = mask * get(grad, pl.ds(k, count, stride=STRIDE))
        total = total + jnp.sum(value, axis=0, keepdims=True)
        frames[:, k * chans : (k + 1) * chans] = value.astype(BF)
    bias_out[6:7, :] = total


def up_backward_kernel(
    sm, frames, e_mine, e_other, up_own, u0, u1, u2, u3, latent_grad, pack, up_weight, pad, up_sem
):
    y = sm[0]
    copies = assemble(sm, up_weight, up_own.shape[1], (up_own,), (u0, u1, u2, u3), up_sem)
    width = e_other.shape[1] // 2
    low, high = halves(y, e_mine[y, :, :width].astype(F32), e_other[:, :width].astype(F32))
    e = jnp.concatenate([low, high], axis=1)
    before = shift_down(pad, e).astype(BF)
    e = e.astype(BF)
    chans = up_weight.shape[1]
    half = chans // 2
    for copy in copies:
        copy.wait()
    now, following = None, None
    for k in range(STRIDE):
        u = frames[:, k * chans : (k + 1) * chans]
        a = dot_nn(u, up_weight[k])
        b = dot_nn(u, up_weight[STRIDE + k])
        now = a if now is None else now + a
        following = b if following is None else following + b
        for index, x in ((k, e), (STRIDE + k, before)):
            value = dot_tn(u, x).astype(BF)
            pack[0, index] = value[:half]
            pack[1, index] = value[half:]
    latent_grad[...] = now + shift_up(pad, following)


def down_forward_kernel(
    sm, frames, bias, down_own, d0, d1, d2, d3, latent, sent, weight, pad, sem
):
    copies = assemble(sm, weight, down_own.shape[1], (down_own,), (d0, d1, d2, d3), sem)
    for copy in copies:
        copy.wait()
    rows, wide = frames.shape
    chans = wide // STRIDE
    now, following = None, None
    for k in range(STRIDE):
        f = frames[:, k * chans : (k + 1) * chans]
        a = dot_nt(f, weight[k])
        b = dot_nt(f, weight[STRIDE + k])
        now = a if now is None else now + a
        following = b if following is None else following + b
    both = jnp.concatenate([bias[13:14, :], bias[14:15, :]], axis=1)
    value = now + shift_up(pad, following) + both
    value = row_mask(0, rows, sm[2]) * value
    latent[...] = value
    group = value.shape[1] // 2
    sent[...] = jnp.where(sm[0] == 0, value[:, group:], value[:, :group]).astype(BF)


def down_backward_kernel(
    sm, latent_grad, latent, e_mine, e_other, frames, down_own, d0, d1, d2, d3,
    frames_grad, pack, bias_out, weight, pad, sem,
):
    y = sm[0]
    copies = assemble(sm, weight, down_own.shape[1], (down_own,), (d0, d1, d2, d3), sem)
    rows = latent.shape[0]
    width = e_other.shape[1] // 2
    mine = e_mine[y].astype(F32)
    other = e_other[...].astype(F32)
    low, high = halves(y, mine, other)
    e = jnp.concatenate([low[:, :width], high[:, :width]], axis=1)
    centre = jnp.concatenate([low[:, width:], high[:, width:]], axis=1)
    mask = row_mask(0, rows, sm[2])
    value = latent_grad[...] * slope(e) + (4.0 * BETA) * (latent[...] - centre)
    value = mask * value
    sums = jnp.sum(value, axis=0, keepdims=True)
    group = sums.shape[1] // 2
    bias_out[...] = jnp.zeros(bias_out.shape, F32)
    bias_out[0:1, :] = sums[:, :group]
    bias_out[1:2, :] = sums[:, group:]
    v = value.astype(BF)
    before = shift_down(pad, v.astype(F32)).astype(BF)
    chans = weight.shape[2]
    for copy in copies:
        copy.wait()
    for k in range(STRIDE):
        at = slice(k * chans, (k + 1) * chans)
        frames_grad[:, at] = dot_nn(v, weight[k]) + dot_nn(before, weight[STRIDE + k])
        f = frames[:, at]
        for index, x in ((k, v), (STRIDE + k, before)):
            part = dot_tn(x, f).astype(BF)
            pack[0, index] = part[:group]
            pack[1, index] = part[group:]


def codebook_kernel(sm, codes, quants, latent, received, out):
    y = sm[0]
    count = out.shape[1]
    frames = codes.shape[-1]
    group = received.shape[1]
    ids = lax.broadcasted_iota(jnp.int32, (count, frames), 0)
    own = jnp.where(y == 0, latent[:, :group], latent[:, group:])
    other = received[...].astype(F32)
    sums = [None, None]
    for clip in range(2):
        residual = jnp.where(y == clip, own, other)
        mask = row_mask(0, frames, sm[3 + clip])
        for level in range(LEVELS):
            quant = quants[clip, level]
            value = (2.0 * mask * (quant - residual)).astype(BF)
            hot = jnp.where(ids == codes[clip, level : level + 1, :], 1.0, 0.0).astype(BF)
            part = dot_nn(hot, value)
            sums[level] = part if clip == 0 else sums[level] + part
            residual = residual - quant
    for level in range(LEVELS):
        out[level] = sums[level].astype(BF)


def encoder_backward_kernel(
    sm, frames_grad, frames, acts, seconds, wide, point, p0, p1, p2, p3,
    pack, bias_out, own, sent, weight, grad, low_out, low_in, sem,
):
    y, limit = sm[0], STRIDE * sm[2]
    copies = assemble(sm, weight, wide.shape[1], (wide, point), (p0, p1, p2, p3), sem)
    _, length, half = grad.shape
    chans = 2 * half
    count = frames.shape[0]
    for k in range(STRIDE):
        at = slice(k * chans, (k + 1) * chans)
        put(grad, pl.ds(k, count, stride=STRIDE), frames_grad[:, at] * slope(frames[:, at]))
    zero_halo(low_in, length)
    bias_out[...] = jnp.zeros(bias_out.shape, F32)
    for copy in copies:
        copy.wait()
    for u in reversed(range(UNITS)):
        unit_backward(u, limit, grad, weight, acts, seconds, low_out, low_in, pack, bias_out)
    for block in range(length // BLOCK):
        at = pl.ds(block * BLOCK, BLOCK)
        mask = row_mask(block * BLOCK, BLOCK, limit)
        mine, other = halves(y, (mask * grad[0, at, :]).T, (mask * grad[1, at, :]).T)
        own[:, at] = mine
        sent[:, at] = other.astype(BF)


def call(kernel, outs, scratch, spaces, *args):
    table = {
        "s": pl.BlockSpec(memory_space=pltpu.SMEM),
        "v": pl.BlockSpec(memory_space=pltpu.VMEM),
        "h": pl.BlockSpec(memory_space=pl.ANY),
    }
    return pl.pallas_call(
        kernel,
        out_shape=tuple(jax.ShapeDtypeStruct(shape, dtype) for shape, dtype in outs),
        in_specs=[table[space] for space in spaces],
        out_specs=tuple(table["v"] for _ in outs),
        scratch_shapes=scratch,
        name=kernel.__name__,
    )(*args)


def shards(
    size,
    audio, lengths, codes, enc_wide, enc_wide_bias, enc_point, enc_point_bias,
    down_weight, down_bias, codebooks, up_weight, up_bias,
    dec_wide, dec_wide_bias, dec_point, dec_point_bias, cotangent,
):
    y = lax.axis_index("chan")
    b = lax.axis_index("batch")
    core, xbit = b & 1, (b >> 1) & 1
    q = 2 * core + xbit
    _, half, length = audio.shape
    chans = 2 * half
    rows = length // STRIDE
    group = down_weight.shape[1]
    latents = 2 * group

    def over_chan(v):
        return lax.ppermute(v, "chan", [(0, 1), (1, 0)])

    def over_batch(v, bit):
        return lax.ppermute(v, "batch", [(i, i ^ bit) for i in range(size)])

    def pick(v, index, axis=0):
        return lax.dynamic_index_in_dim(v, index, axis, keepdims=False)

    def fetch(w):
        n, count, cols = w.shape
        mine = pick(w.reshape(n, 4, count // 4, cols), q, 1)
        p0 = over_chan(mine)
        p1 = over_batch(p0, 2)
        return p0, p1, over_batch(p0, 1), over_batch(p1, 1)

    sm = jnp.stack([y, q, pick(lengths, y), lengths[0], lengths[1]]).astype(jnp.int32)

    def fetch_unit(wide, point):
        wide = wide.reshape(UNITS * TAPS, half, chans)
        return (wide, point) + fetch(jnp.concatenate([wide, point], axis=0))

    biases = jnp.concatenate(
        [
            enc_wide_bias, enc_point_bias, dec_wide_bias, dec_point_bias,
            up_bias[None], down_bias.reshape(2, half),
        ],
        axis=0,
    ).astype(F32)
    biases_other = over_chan(biases)
    low, high = halves(y, biases, biases_other)
    bias = jnp.concatenate(
        [jnp.concatenate([low, high], axis=1)[:13], low[13:].reshape(1, group), high[13:].reshape(1, group)],
        axis=0,
    )

    audio_other = over_chan(pick(audio, 1 - y))
    enc_weights = fetch_unit(enc_wide, enc_point)

    codes = codes[:, 0]
    quants, values = call(
        lookup_kernel,
        [((2, LEVELS, rows, group), F32), ((2, rows, 2 * group), BF)],
        [],
        "svv",
        sm, codes, codebooks[0],
    )
    values_other = over_chan(pick(values, 1 - y))

    up_weights = (up_weight,) + fetch(up_weight)
    dec_weights = fetch_unit(dec_wide, dec_point)
    cot_other = over_chan(pick(cotangent, 1 - y))
    down_weights = (down_weight,) + fetch(down_weight)

    unit_scratch = pltpu.VMEM((UNITS * (TAPS + 1), chans, chans), BF)
    up_scratch = pltpu.VMEM((2 * STRIDE, chans, latents), BF)
    down_scratch = pltpu.VMEM((2 * STRIDE, latents, chans), BF)
    stream = pltpu.VMEM((2, length, half), F32)
    low_plain = pltpu.VMEM((length, chans), BF)
    low_padded = pltpu.VMEM((length + 2 * HALO, chans), BF)
    pad = pltpu.VMEM((rows + 8, latents), F32)
    six = pltpu.SemaphoreType.DMA((6,))
    five = pltpu.SemaphoreType.DMA((5,))
    kept = [
        ((UNITS, length + 2 * HALO, chans), BF),
        ((UNITS, length, chans), BF),
    ]
    unit_pack = ((2, UNITS * (TAPS + 1), half, chans), BF)

    enc_acts, enc_seconds, frames = call(
        encoder_forward_kernel,
        kept + [((rows, STRIDE * chans), BF)],
        [unit_scratch, stream, six],
        "svvv" + "hhhhhh",
        sm, audio, audio_other, bias, *enc_weights,
    )
    dec_acts, dec_seconds, out_own, out_sent = call(
        decoder_forward_kernel,
        kept + [((half, length), BF), ((half, length), BF)],
        [up_scratch, unit_scratch, stream, pad, five, six],
        "svvv" + "hhhhh" + "hhhhhh",
        sm, values, values_other, bias, *up_weights, *dec_weights,
    )
    out_other = over_chan(out_sent)
    latent, latent_sent = call(
        down_forward_kernel,
        [((rows, latents), F32), ((rows, group), BF)],
        [down_scratch, pad, five],
        "svv" + "hhhhh",
        sm, frames, bias, *down_weights,
    )
    latent_other = over_chan(latent_sent)
    dec_pack, dec_bias_grad, up_frames = call(
        decoder_backward_kernel,
        [unit_pack, ((8, chans), F32), ((rows, STRIDE * chans), BF)],
        [unit_scratch, stream, low_plain, low_padded, six],
        "svvvv" + "hhhhhh",
        sm, cotangent, cot_other, dec_acts, dec_seconds, *dec_weights,
    )
    latent_grad, up_pack = call(
        up_backward_kernel,
        [((rows, latents), F32), ((2, 2 * STRIDE, half, latents), BF)],
        [up_scratch, pad, five],
        "svvv" + "hhhhh",
        sm, up_frames, values, values_other, *up_weights,
    )
    (book_pack,) = call(
        codebook_kernel,
        [((LEVELS, codebooks.shape[2], group), BF)],
        [],
        "svvvv",
        sm, codes, quants, latent, latent_other,
    )
    frames_grad, down_pack, down_bias_grad = call(
        down_backward_kernel,
        [((rows, STRIDE * chans), F32), ((2, 2 * STRIDE, group, chans), BF), ((8, group), F32)],
        [down_scratch, pad, five],
        "svvvvv" + "hhhhh",
        sm, latent_grad, latent, values, values_other, frames, *down_weights,
    )
    enc_pack, enc_bias_grad, grad_own, grad_sent = call(
        encoder_backward_kernel,
        [unit_pack, ((8, chans), F32), ((half, length), F32), ((half, length), BF)],
        [unit_scratch, stream, low_plain, low_padded, six],
        "svvvv" + "hhhhhh",
        sm, frames_grad, frames, enc_acts, enc_seconds, *enc_weights,
    )
    grad_other = over_chan(grad_sent)

    def by_clip(own, other, dtype):
        own, other = own.astype(dtype), other.astype(dtype)
        return jnp.where(y == 0, jnp.stack([own, other]), jnp.stack([other, own]))

    def add(a, c):
        return (a.astype(F32) + c.astype(F32)).astype(BF)

    def reduce(pack, split):
        parts = 2 if split else 1
        pieces = pack.reshape(parts, size // 2, 2, -1, chans)
        value = add(pick(pieces, core, 2), over_batch(pick(pieces, 1 - core, 2), 1))
        if split:
            value = add(pick(value, y), over_chan(pick(value, 1 - y)))
        else:
            value = value[0]
        bit = 2
        while bit < size:
            mine = (b // bit) & 1
            value = value.reshape(value.shape[0] // 2, 2, *value.shape[1:]) if bit == 2 else value
            if bit > 2:
                value = value.reshape(value.shape[0] // 2, 2, *value.shape[1:])
            value = add(pick(value, mine, 1), over_batch(pick(value, 1 - mine, 1), bit))
            bit *= 2
        return lax.all_gather(value.reshape(-1, chans), "batch", axis=0, tiled=True).astype(F32)

    dec_sum = reduce(dec_pack, True)
    up_sum = reduce(up_pack, True)
    book_sum = reduce(book_pack, False)
    down_sum = reduce(down_pack, True)
    enc_sum = reduce(enc_pack, True)

    def reduce_bias(v):
        v = v + over_chan(v)
        bit = 1
        while bit < size:
            v = v + over_batch(v, bit)
            bit *= 2
        return v

    bias_sum = reduce_bias(jnp.concatenate([dec_bias_grad, enc_bias_grad, down_bias_grad], axis=0))
    mine = pick(bias_sum.reshape(-1, 2, half), y, 1)

    def unit_grads(total):
        wide = total[: UNITS * TAPS * half].reshape(UNITS, TAPS, half, chans)
        return wide, total[UNITS * TAPS * half :].reshape(UNITS, half, chans)

    enc_wide_grad, enc_point_grad = unit_grads(enc_sum)
    dec_wide_grad, dec_point_grad = unit_grads(dec_sum)
    return (
        by_clip(out_own, out_other, BF),
        by_clip(grad_own, grad_other, F32),
        enc_wide_grad,
        mine[8:11],
        enc_point_grad,
        mine[11:14],
        down_sum.reshape(2 * STRIDE, group, chans),
        pick(bias_sum, 16 + y),
        book_sum.reshape(1, LEVELS, -1, group),
        up_sum.reshape(2 * STRIDE, half, latents),
        mine[6],
        dec_wide_grad,
        mine[0:3],
        dec_point_grad,
        mine[3:6],
    )


def solution(mesh):
    placed = (
        P("batch", "chan", None),
        P("batch"),
        P("batch", "chan", None, None),
        P(None, None, "chan", None),
        P(None, "chan"),
        P(None, "chan", None),
        P(None, "chan"),
        P(None, "chan", None),
        P("chan"),
        P("chan", None, None, None),
        P(None, "chan", None),
        P("chan"),
        P(None, None, "chan", None),
        P(None, "chan"),
        P(None, "chan", None),
        P(None, "chan"),
        P("batch", "chan", None),
    )
    return jax.shard_map(
        functools.partial(shards, mesh.shape["batch"]),
        mesh=mesh,
        in_specs=placed,
        out_specs=(
            P("batch", "chan", None),
            P("batch", "chan", None),
            P(None, None, "chan", None),
            P(None, "chan"),
            P(None, "chan", None),
            P(None, "chan"),
            P(None, "chan", None),
            P("chan"),
            P("chan", None, None, None),
            P(None, "chan", None),
            P("chan"),
            P(None, None, "chan", None),
            P(None, "chan"),
            P(None, "chan", None),
            P(None, "chan"),
        ),
        check_vma=False,
    )
```
